32 devices in a mesh: rep: 4 (over y, core), shard: 8 (over z, x).
Axes of the slice: x: 2, y: 2, z: 4, core: 2. Of those that a mesh axis runs over, the one named last changes fastest.
Arguments:
- inputs: bfloat16 [32768, 768], P(('rep', 'shard')), may hold values from -6 to 6
- cotangent: bfloat16 [32768, 768], P(('rep', 'shard')), may hold values from -6 to 6
- segment_ids: int32 [32, 1024], P(('rep', 'shard')), may hold values from 0 to 15, never falling along the last dimension, each value on 1 to 512 neighbouring positions
- random_blocks: int32 [32, 16, 3], P(('rep', 'shard')), may hold values from 0 to 15
- qkv_weight: bfloat16 [3, 768, 768], P(None, 'shard'), may hold values from -0.21875 to 0.21875
- out_weight: bfloat16 [768, 768], P('shard'), may hold values from -0.875 to 0.875
- up_weight: bfloat16 [768, 3072], P('shard'), may hold values from -0.21875 to 0.21875
- down_weight: bfloat16 [3072, 768], P('shard'), may hold values from -0.109375 to 0.109375
- vectors: bfloat16 [8, 768], P(None, 'shard'), may hold values from -1.75 to 1.75
- ffn_bias: bfloat16 [3072], P('shard'), may hold values from -1.75 to 1.75
- qkv_moment: float32 [3, 768, 768], P(None, 'shard'), may hold values from -320 to 320
- out_moment: float32 [768, 768], P('shard'), may hold values from -320 to 320
- up_moment: float32 [768, 3072], P('shard'), may hold values from -320 to 320
- down_moment: float32 [3072, 768], P('shard'), may hold values from -320 to 320
- vector_moment: float32 [8, 768], P(None, 'shard'), may hold values from -320 to 320
- ffn_bias_moment: float32 [3072], P('shard'), may hold values from -320 to 320
Outputs:
- outputs: bfloat16 [32768, 768], P(('rep', 'shard'))
- input_grad: float32 [32768, 768], P(('rep', 'shard'))
- qkv_grad: float32 [3, 768, 768], P(None, 'shard')
- out_grad: float32 [768, 768], P('shard')
- up_grad: float32 [768, 3072], P('shard')
- down_grad: float32 [3072, 768], P('shard')
- vector_grad: float32 [8, 768], P(None, 'shard')
- ffn_bias_grad: float32 [3072], P('shard')
- qkv_moment_new: float32 [3, 768, 768], P(None, 'shard')
- out_moment_new: float32 [768, 768], P('shard')
- up_moment_new: float32 [768, 3072], P('shard')
- down_moment_new: float32 [3072, 768], P('shard')
- vector_moment_new: float32 [8, 768], P(None, 'shard')
- ffn_bias_moment_new: float32 [3072], P('shard')
- qkv_update: float32 [3, 768, 768], P(None, 'shard')
- out_update: float32 [768, 768], P('shard')
- up_update: float32 [768, 3072], P('shard')
- down_update: float32 [3072, 768], P('shard')
- vector_update: float32 [8, 768], P(None, 'shard')
- ffn_bias_update: float32 [3072], P('shard')
The draws below stay inside these ranges and needn't reach their ends.
Inputs may be any that keep to these rules, and one draw needn't show every extreme that they name: `segment_ids`: within a sequence the numbers never fall; one document has at most 512 tokens.
All inputs are finite; a program needn't handle non-finite values.
Results may differ from the reference program's by a relative error of at most 0.022.
Values may be sent and summed in bfloat16 or wider, within the bound.
No kernel may reach another device: no remote copies, remote signals or barrier semaphores. Data moves between devices by JAX's collectives and lax.ppermute only.
A program may use at most 384 MiB of HBM per device.

```python
import math
import jax
import jax.numpy as jnp
import numpy as np
from jax import lax

D = 768
H = 12
HD = 64
FF = 3072
LEN = 1024
BLK = 64
RND = 3
NB = 16
SEQS = 32
TOKENS = 32768


def place_ends(drawn, stream_key, least, top_value):
    extent = drawn.shape
    spot = [jax.random.randint(jax.random.fold_in(stream_key, axis), (), 0, extent[axis]) for axis in range(len(extent))]
    drawn = drawn.at[tuple(spot)].set(least)
    longest = extent.index(max(extent))
    spot[longest] = (spot[longest] + 1) % extent[longest]
    return drawn.at[tuple(spot)].set(top_value)


def level_of(stream_key, dims, split, low, largest):
    factor_of, own = 1.0, jax.random.fold_in(stream_key, 6)
    for position, shards_of in split:
        steps = jnp.exp(jax.random.uniform(jax.random.fold_in(own, position), (shards_of,), jnp.float32, low / len(split), largest / len(split)))
        factor_of = factor_of * jnp.repeat(steps, dims[position] // shards_of).reshape([-1 if axis == position else 1 for axis in range(len(dims))])
    return factor_of


def split_up(amount, total, bound, skew):
    portions = [(1 << 20) // math.isqrt(grade ** skew) + 1 for grade in range(2, amount + 1)]
    surplus, given = total - bound - (amount - 1), [1] * (amount - 1)
    while surplus > 0:
        free = [i for i in range(amount - 1) if given[i] < bound]
        whole, budget = sum([portions[i] for i in free]), surplus
        for i in free:
            addition = min(bound - given[i], max(1, budget * portions[i] // whole), surplus)
            given[i] = given[i] + addition
            surplus = surplus - addition
    return np.array([bound] + given)


def uneven(stream_key, amount, total, bound, skew):
    if amount == 2:
        one = jax.random.randint(stream_key, (), max(1, total - bound), min(bound, total - 1) + 1)
        return jnp.stack([one, total - one])
    tallies = jnp.asarray(split_up(amount, total, bound, skew), jnp.int32)
    couples = (amount - 1) // 2
    source_of, sink = tallies[1:1 + 2 * couples:2], tallies[2:2 + 2 * couples:2]
    margin = jnp.minimum(source_of - 1, bound - sink)
    shifted = jax.random.randint(jax.random.fold_in(stream_key, 1), (couples,), 0, 1 << 20) % (margin + 1)
    tallies = tallies.at[1:1 + 2 * couples:2].set(source_of - shifted).at[2:2 + 2 * couples:2].set(sink + shifted)
    return tallies[jax.random.permutation(jax.random.fold_in(stream_key, 2), amount)]


def normal_values(key, extent, width, most, pieces=(), held_as=jnp.bfloat16):
    loudness = level_of(key, extent, pieces, -0.22, 0.18) if pieces else 1.0
    drawn = jax.random.normal(key, extent, jnp.float32) * width * loudness
    return jnp.minimum(jnp.maximum(drawn, -most), most).astype(held_as)


def setup_inputs(seed: int = 0) -> dict:
    seeds = jax.random.split(jax.random.key(seed), 17)
    return {
        "inputs": normal_values(seeds[0], (TOKENS, D), 1.0, 6.0, ((0, 32),)),
        "cotangent": normal_values(seeds[1], (TOKENS, D), 1.0, 6.0, ((0, 32),)),
        "segment_ids": jax.vmap(lambda own: jnp.searchsorted(jnp.cumsum(uneven(own, NB, LEN, LEN // 2, 2)), jnp.arange(LEN), side="right"))(jax.random.split(seeds[2], SEQS)).reshape((SEQS, LEN)).astype(jnp.int32),
        "random_blocks": place_ends(jax.random.randint(seeds[3], (SEQS, NB, RND), 0, NB), jax.random.fold_in(seeds[3], 1), 0, NB - 1).astype(jnp.int32),
        "qkv_weight": normal_values(seeds[4], (3, D, D), D ** -0.5, 0.21875, ((1, 8),)),
        "out_weight": normal_values(seeds[5], (D, D), (D // 16) ** -0.5, 0.875, ((0, 8),)),
        "up_weight": normal_values(seeds[6], (D, FF), D ** -0.5, 0.21875, ((0, 8),)),
        "down_weight": normal_values(seeds[7], (FF, D), FF ** -0.5, 0.109375, ((0, 8),)),
        "vectors": normal_values(seeds[8], (8, D), 0.3, 1.75, ((1, 8),)),
        "ffn_bias": normal_values(seeds[9], (FF,), 0.3, 1.75, ((0, 8),)),
        "qkv_moment": normal_values(seeds[10], (3, D, D), (0.3 * TOKENS ** 0.5), 320.0, ((1, 8),), jnp.float32),
        "out_moment": normal_values(seeds[11], (D, D), (0.3 * TOKENS ** 0.5), 320.0, ((0, 8),), jnp.float32),
        "up_moment": normal_values(seeds[12], (D, FF), (0.3 * TOKENS ** 0.5), 320.0, ((0, 8),), jnp.float32),
        "down_moment": normal_values(seeds[13], (FF, D), (0.3 * TOKENS ** 0.5), 320.0, ((0, 8),), jnp.float32),
        "vector_moment": normal_values(seeds[14], (8, D), (0.3 * TOKENS ** 0.5), 320.0, ((1, 8),), jnp.float32),
        "ffn_bias_moment": normal_values(seeds[15], (FF,), (0.3 * TOKENS ** 0.5), 320.0, ((0, 8),), jnp.float32),
    }


@jax.custom_vjp
def low(v):
    return lax.optimization_barrier(v.astype(jnp.bfloat16)).astype(jnp.float32)

@jax.custom_vjp
def low_back(v):
    return v

def low_keep(v):
    return (low(v), None)

def low_pass(kept, grad):
    return (grad,)

def back_keep(v):
    return (v, None)

def back_low(kept, grad):
    return (low(grad),)
low.defvjp(low_keep, low_pass)
low_back.defvjp(back_keep, back_low)
HIGHEST = lax.Precision.HIGHEST
EPS = 1e-06
MASKED_SCORE = -1e+30
COEF_A = 3.4445
COEF_B = -4.775
COEF_C = 2.0315
MOMENTUM = 0.5
MATRIX_RATE = 0.8
VECTOR_RATE = 0.0005

def matmul(left, right):
    return jnp.dot(left, right, precision=HIGHEST)

def normalize(residual, gain_row, shift_row):
    row_mean = lax.optimization_barrier(jnp.mean(residual, axis=-1, keepdims=True))
    centered = residual - row_mean
    variance = lax.optimization_barrier(jnp.mean(centered * centered, axis=-1, keepdims=True))
    return centered * lax.rsqrt(variance + EPS) * (1.0 + gain_row) + shift_row

def token_mask(segments, chosen_blocks):
    block_ids = jnp.arange(NB, dtype=jnp.int32)
    chosen = jnp.any(chosen_blocks[:, :, None] == block_ids[None, None, :], axis=1)
    adjacent = jnp.abs(block_ids[:, None] - block_ids[None, :]) <= 1
    allowed_blocks = chosen | adjacent
    block_of = jnp.arange(LEN, dtype=jnp.int32) // BLK
    allowed = allowed_blocks[block_of[:, None], block_of[None, :]]
    return allowed & (segments[:, None] == segments[None, :])

def layer(params, tokens_in, allowed):
    w_qkv, w_out, w_up, w_down, vec_rows, bias_ff = params
    scaling = HD ** (-0.5)
    queries = low_back(low(matmul(tokens_in, w_qkv[0]) + vec_rows[0])).reshape(LEN, H, HD)
    key_rows = low_back(low(matmul(tokens_in, w_qkv[1]))).reshape(LEN, H, HD)
    value_rows = low_back(low(matmul(tokens_in, w_qkv[2]) + vec_rows[1])).reshape(LEN, H, HD)
    scores = jnp.einsum('qhd,khd->hqk', queries, key_rows, precision=HIGHEST) * scaling
    scores = low_back(jnp.where(allowed[None], scores, MASKED_SCORE))
    probability = jax.nn.softmax(scores, axis=-1)
    context = jnp.einsum('hqk,khd->qhd', low(probability), value_rows, precision=HIGHEST).reshape(LEN, D)
    context = low_back(low(context))
    attended = low_back(matmul(context, w_out) + vec_rows[2])
    hidden = normalize(tokens_in + attended, vec_rows[3], vec_rows[4])
    pre_act = low_back(matmul(low(hidden), w_up) + bias_ff)
    activated = jax.nn.gelu(pre_act, approximate=False)
    mlp_out = low_back(matmul(low(activated), w_down) + vec_rows[5])
    return normalize(hidden + mlp_out, vec_rows[6], vec_rows[7])

def orthogonal_step(moment):
    height, breadth = moment.shape
    oriented = moment if height <= breadth else moment.T
    frob_norm = jnp.sqrt(jnp.sum(moment * moment))
    iterate = oriented / (frob_norm + 1e-07)
    for iteration in range(5):
        gram = jnp.dot(iterate, iterate.T, precision=HIGHEST)
        squared = jnp.dot(gram, gram, precision=HIGHEST)
        mixer = COEF_B * gram + COEF_C * squared
        iterate = COEF_A * iterate + jnp.dot(mixer, iterate, precision=HIGHEST)
    ortho = iterate
    if height > breadth:
        ortho = ortho.T
    return -MATRIX_RATE * math.sqrt(max(1.0, height / breadth)) * ortho

def reference(inputs, cotangent, segment_ids, random_blocks, qkv_weight, out_weight, up_weight, down_weight, vectors, ffn_bias, qkv_moment, out_moment, up_moment, down_moment, vector_moment, ffn_bias_moment):
    params = tuple((weight.astype(jnp.float32) for weight in (qkv_weight, out_weight, up_weight, down_weight, vectors, ffn_bias)))
    tokens_all = inputs.astype(jnp.float32).reshape(SEQS, LEN, D)
    cotangent_all = cotangent.astype(jnp.float32).reshape(SEQS, LEN, D)

    def one_sequence(running, element):
        tokens_in, grad_out, segments, chosen_blocks = element
        allowed = token_mask(segments, chosen_blocks)
        result, pullback = jax.vjp(lambda weights, tokens: layer(weights, tokens, allowed), params, tokens_in)
        grad_params, grad_tokens = pullback(grad_out)
        running = jax.tree.map(lambda left, right: left + right, running, grad_params)
        return (running, (result.astype(jnp.bfloat16), grad_tokens))
    initial = jax.tree.map(jnp.zeros_like, params)
    grads, (outputs, input_grad) = lax.scan(one_sequence, initial, (tokens_all, cotangent_all, segment_ids, random_blocks))
    qkv_grad, out_grad, up_grad, down_grad, vector_grad, ffn_bias_grad = grads
    qkv_new = MOMENTUM * qkv_moment + qkv_grad
    out_new = MOMENTUM * out_moment + out_grad
    up_new = MOMENTUM * up_moment + up_grad
    down_new = MOMENTUM * down_moment + down_grad
    vector_new = MOMENTUM * vector_moment + vector_grad
    ffn_new = MOMENTUM * ffn_bias_moment + ffn_bias_grad
    qkv_update = jnp.stack([orthogonal_step(qkv_new[slot]) for slot in range(3)])
    out_update = orthogonal_step(out_new)
    up_update = orthogonal_step(up_new)
    down_update = orthogonal_step(down_new)
    vector_update = -VECTOR_RATE * vector_new
    ffn_bias_update = -VECTOR_RATE * ffn_new
    return (outputs.reshape(TOKENS, D), input_grad.reshape(TOKENS, D), qkv_grad, out_grad, up_grad, down_grad, vector_grad, ffn_bias_grad, qkv_new, out_new, up_new, down_new, vector_new, ffn_new, qkv_update, out_update, up_update, down_update, vector_update, ffn_bias_update)
```

```python
import math

import jax
import jax.numpy as jnp
from jax import lax
from jax.experimental import pallas as pl
from jax.experimental.pallas import tpu as pltpu
from jax.sharding import PartitionSpec as P

D = 768
H = 12
HD = 64

EPS = 1e-06
MASKED_SCORE = -1e30
COEF_A = 3.4445
COEF_B = -4.775
COEF_C = 2.0315
MOMENTUM = 0.5
MATRIX_RATE = 0.8
VECTOR_RATE = 0.0005
SQRT_HALF = 0.7071067811865476
DENSITY_SCALE = 0.3989422804014327
BF = jnp.bfloat16
F32 = jnp.float32


def flip(values, axis, bit):
    size = lax.axis_size(axis)
    return lax.ppermute(values, axis, [(i, i ^ bit) for i in range(size)])


def shard_bits():
    bits, bit = [], lax.axis_size("shard") // 2
    while bit:
        bits.append(bit)
        bit //= 2
    return bits


def bit_of(axis, bit):
    return lax.rem(lax.div(lax.axis_index(axis), bit), 2)


def shard_gather(values):
    held, shape = values[None], values.shape
    for bit in shard_bits():
        other, low = flip(held, "shard", bit), bit_of("shard", bit) == 0
        held = jnp.stack([jnp.where(low, held, other), jnp.where(low, other, held)], axis=1)
        held = held.reshape((-1,) + shape)
    return held


def shard_reduce(blocks):
    shape = blocks.shape[1:]
    for bit in reversed(shard_bits()):
        pairs = blocks.reshape((-1, 2) + shape)
        mine = bit_of("shard", bit)
        send = lax.dynamic_index_in_dim(pairs, 1 - mine, 1, keepdims=False).astype(BF)
        keep = lax.dynamic_index_in_dim(pairs, mine, 1, keepdims=False)
        blocks = keep.astype(F32) + flip(send, "shard", bit).astype(F32)
    return blocks[0]


def rep_bits():
    bits, bit = [], 2
    while bit < lax.axis_size("rep"):
        bits.append(bit)
        bit *= 2
    return bits


def rest_sum(values):
    for bit in rep_bits():
        low = values.astype(BF)
        values = low.astype(F32) + flip(low, "rep", bit).astype(F32)
    return values


def all_sum(values):
    for bit in [1] + rep_bits():
        values = values + flip(values, "rep", bit)
    bit = 1
    while bit < lax.axis_size("shard"):
        values = values + flip(values, "shard", bit)
        bit *= 2
    return values


def reduce_halves(mine, other):
    summed = mine.astype(F32) + flip(other, "rep", 1).astype(F32)
    half = rest_sum(shard_reduce(summed.astype(BF)))
    return half, flip(half, "rep", 1)


NT = (((1,), (1,)), ((), ()))
NN = (((1,), (0,)), ((), ()))
TN = (((0,), (0,)), ((), ()))
NS_TILE = 256


def newton_schulz(source, inverse, wide, low, gram_low, mix_low, gram):
    n, c = wide.shape
    tiles = [slice(b * NS_TILE, (b + 1) * NS_TILE) for b in range(n // NS_TILE)]
    rows = lax.broadcasted_iota(jnp.int32, (NS_TILE, n), 0)
    cols = lax.broadcasted_iota(jnp.int32, (NS_TILE, n), 1)
    chunk = min(c, 768)

    def iteration(_, carry):
        dcols, drow = [], jnp.zeros((1, n), F32)
        for tile in tiles:
            acc = lax.dot_general(low[tile, :], low[...], NT, preferred_element_type=F32)
            diagonal = jnp.where(cols == rows + tile.start, acc, 0.0)
            dcols.append(jnp.sum(diagonal, axis=1, keepdims=True))
            drow = drow + jnp.sum(diagonal, axis=0, keepdims=True)
            off = acc - diagonal
            gram[tile, :] = off
            gram_low[tile, :] = off.astype(BF)
        own = []
        for tile, dcol in zip(tiles, dcols):
            off = gram[tile, :]
            square = lax.dot_general(gram_low[tile, :], gram_low[...], NN, preferred_element_type=F32)
            mixed = COEF_C * square + (COEF_B + COEF_C * (dcol + drow)) * off
            eye = cols == rows + tile.start
            extra = jnp.sum(jnp.where(eye, mixed, 0.0), axis=1, keepdims=True)
            own.append(COEF_A + extra + COEF_B * dcol + COEF_C * dcol * dcol)
            mix_low[tile, :] = jnp.where(eye, 0.0, mixed).astype(BF)
        for k in range(c // chunk):
            part = slice(k * chunk, (k + 1) * chunk)
            sums = [
                lax.dot_general(mix_low[tile, :], low[:, part], NN, preferred_element_type=F32)
                for tile in tiles
            ]
            for tile, scale, total in zip(tiles, own, sums):
                value = scale * wide[tile, part] + total
                wide[tile, part] = value
                low[tile, part] = value.astype(BF)
        return carry

    lax.fori_loop(0, 5, iteration, 0)


def norm_inverse(values_of, count):
    total = lax.fori_loop(
        0,
        count,
        lambda i, held: held + jnp.sum(jnp.square(values_of(i).astype(F32)), axis=0, keepdims=True),
        jnp.zeros((1, D), F32),
    )
    return 1.0 / (jnp.sqrt(jnp.sum(total)) + 1e-7)


def square_kernel(place, source, result, wide, low, gram_low, mix_low, gram):
    n = source.shape[0]
    inverse = norm_inverse(lambda i: source[pl.ds(pl.multiple_of(i * 64, 64), 64), :], n // 64)

    def begin(i, carry):
        part = pl.ds(pl.multiple_of(i * 64, 64), 64)
        value = source[part, :].astype(F32) * inverse
        wide[part, :] = value
        low[part, :] = value.astype(BF)
        return carry

    lax.fori_loop(0, n // 64, begin, 0)
    newton_schulz(source, inverse, wide, low, gram_low, mix_low, gram)
    height = result.shape[0]
    result[...] = low[pl.ds(pl.multiple_of(place[0] * height, height), height), :]


def square_step(moment, place):
    n = moment.shape[0]
    height = n // lax.axis_size("shard")
    return pl.pallas_call(
        square_kernel,
        out_shape=jax.ShapeDtypeStruct((height, n), BF),
        in_specs=[pl.BlockSpec(memory_space=pltpu.SMEM), pl.BlockSpec(memory_space=pltpu.VMEM)],
        out_specs=pl.BlockSpec(memory_space=pltpu.VMEM),
        scratch_shapes=[
            pltpu.VMEM((n, n), F32),
            pltpu.VMEM((n, n), BF),
            pltpu.VMEM((n, n), BF),
            pltpu.VMEM((n, n), BF),
            pltpu.VMEM((n, n), F32),
        ],
        compiler_params=pltpu.CompilerParams(vmem_limit_bytes=32 * 2**20),
        cost_estimate=pl.CostEstimate(flops=30 * n**3, bytes_accessed=3 * n * n, transcendentals=0),
        name="square_step",
    )(place, moment)


def tall_kernel(info, blocks, result, wide, low, gram_low, mix_low, gram):
    shards, size, n = blocks.shape
    groups = wide.shape[1] // n
    height = size // groups

    def piece(i):
        return blocks[i]

    inverse = norm_inverse(piece, shards)

    @pl.when(info[1] == 0)
    def _():
        for s in range(shards):
            for g in range(groups):
                value = blocks[s, g * height : (g + 1) * height, :].astype(F32) * inverse
                at = (slice(s * height, (s + 1) * height), slice(g * n, (g + 1) * n))
                wide[at] = value
                low[at] = value.astype(BF)

    @pl.when(info[1] != 0)
    def _():
        for s in range(shards):
            value = blocks[s].astype(F32).T * inverse
            at = (slice(None), slice(s * size, (s + 1) * size))
            wide[at] = value
            low[at] = value.astype(BF)

    newton_schulz(None, inverse, wide, low, gram_low, mix_low, gram)

    @pl.when(info[1] == 0)
    def _():
        own = pl.ds(pl.multiple_of(info[0] * height, height), height)
        for g in range(groups):
            result[g * height : (g + 1) * height, :] = low[own, g * n : (g + 1) * n]

    @pl.when(info[1] != 0)
    def _():
        own = pl.ds(pl.multiple_of(info[0] * size, 128), size)
        result[...] = wide[:, own].T.astype(BF)


def tall_step(blocks, info):
    shards, size, n = blocks.shape
    c = shards * size
    return pl.pallas_call(
        tall_kernel,
        out_shape=jax.ShapeDtypeStruct((size, n), BF),
        in_specs=[pl.BlockSpec(memory_space=pltpu.SMEM), pl.BlockSpec(memory_space=pltpu.VMEM)],
        out_specs=pl.BlockSpec(memory_space=pltpu.VMEM),
        scratch_shapes=[
            pltpu.VMEM((n, c), F32),
            pltpu.VMEM((n, c), BF),
            pltpu.VMEM((n, n), BF),
            pltpu.VMEM((n, n), BF),
            pltpu.VMEM((n, n), F32),
        ],
        compiler_params=pltpu.CompilerParams(vmem_limit_bytes=48 * 2**20),
        cost_estimate=pl.CostEstimate(
            flops=10 * n * n * (2 * c + n), bytes_accessed=3 * n * c, transcendentals=0
        ),
        name="tall_step",
    )(info, blocks)


Q_TILE = 128
K_TILE = 256


def mask_tile(seg_keys, seg_row, bits_row, first_block, block):
    parts = []
    for sub in range(K_TILE // block):
        open_row = lax.bitwise_and(lax.shift_right_logical(bits_row, first_block + sub), 1)
        target = jnp.where(open_row > 0, seg_row, -1)
        keys = seg_keys[sub * block : (sub + 1) * block, :]
        parts.append(jnp.where(keys == target, 0.0, MASKED_SCORE))
    return jnp.concatenate(parts, axis=0)


def two_heads(pair):
    blank = jnp.zeros((HD, pair.shape[1]), pair.dtype)
    top, bottom = pair[:HD], pair[HD:]
    return jnp.concatenate(
        [jnp.concatenate([top, blank], axis=0), jnp.concatenate([blank, bottom], axis=0)], axis=1
    )


def own_columns(product):
    n = product.shape[1] // 2
    return jnp.concatenate([product[:HD, :n], product[HD:, n:]], axis=0)


def spread(pair_row):
    n = pair_row.shape[1] // 2
    return jnp.concatenate(
        [jnp.broadcast_to(pair_row[:, :n], (HD, n)), jnp.broadcast_to(pair_row[:, n:], (HD, n))], axis=0
    )


def forward_kernel(flags, q_ref, k_ref, vt_ref, seg_col, seg_row, bits_row, out_ref, outt_ref, lse_ref, qt, top, total, acc):
    step = pl.program_id(0)
    tiles = k_ref.shape[0] // K_TILE
    block = k_ref.shape[0] // 16
    top[...] = jnp.full(top.shape, -jnp.inf, F32)
    total[...] = jnp.zeros(total.shape, F32)
    acc[...] = jnp.zeros(acc.shape, F32)
    turned = (q_ref[...].astype(F32) * HD**-0.5).T.astype(BF)
    for pair in range(H // 2):
        qt[pair] = two_heads(turned[pair * 128 : (pair + 1) * 128])

    def tile(j, carry):
        @pl.when(flags[step * tiles + j] > 0)
        def _():
            keys = pl.ds(pl.multiple_of(j * K_TILE, K_TILE), K_TILE)
            bias = mask_tile(seg_col[keys, :], seg_row[...], bits_row[...], j * (K_TILE // block), block)
            bias = jnp.concatenate([bias, bias], axis=1)
            tops, totals = top[...], total[...]
            new_tops, new_totals = [], []
            for pair in range(H // 2):
                lanes = slice(pair * 128, (pair + 1) * 128)
                scores = jnp.dot(k_ref[keys, lanes], qt[pair], preferred_element_type=F32) + bias
                old = tops[pair : pair + 1, :]
                new = jnp.maximum(old, jnp.max(scores, axis=0, keepdims=True))
                decay = jnp.exp(old - new)
                weights = jnp.exp(scores - new)
                new_tops.append(new)
                new_totals.append(
                    totals[pair : pair + 1, :] * decay + jnp.sum(weights, axis=0, keepdims=True)
                )
                product = jnp.dot(vt_ref[lanes, keys], weights.astype(BF), preferred_element_type=F32)
                acc[lanes, :] = acc[lanes, :] * spread(decay) + own_columns(product)
            filler = [tops[H // 2 :]]
            top[...] = jnp.concatenate(new_tops + filler, axis=0)
            total[...] = jnp.concatenate(new_totals + filler, axis=0)

        return carry

    lax.fori_loop(0, tiles, tile, 0)
    for pair in range(H // 2):
        lanes = slice(pair * 128, (pair + 1) * 128)
        value = acc[lanes, :] / spread(total[pair : pair + 1, :])
        outt_ref[lanes, :] = value.astype(BF)
        out_ref[:, lanes] = value.T.astype(BF)
    lse_ref[...] = top[...] + jnp.log(total[...])


def backward_kernel(
    flags, q_ref, k_ref, kt_ref, v_ref, do_ref, outt_ref, lse_ref, seg_col, seg_row, bits_row,
    dq_ref, dk_ref, dv_ref, qt, dot_ref, q_split, do_split, delta, dqt, dk, dv,
):
    step = pl.program_id(0)
    tiles = k_ref.shape[0] // K_TILE
    block = k_ref.shape[0] // 16

    @pl.when(step == 0)
    def _():
        dk[...] = jnp.zeros(dk.shape, F32)
        dv[...] = jnp.zeros(dv.shape, F32)

    dqt[...] = jnp.zeros(dqt.shape, F32)
    turned = (q_ref[...].astype(F32) * HD**-0.5).T.astype(BF)
    turned_do = do_ref[...].astype(F32).T.astype(BF)
    low_lanes = lax.broadcasted_iota(jnp.int32, (Q_TILE, 128), 1) < HD
    deltas = []
    for pair in range(H // 2):
        lanes = slice(pair * 128, (pair + 1) * 128)
        qt[pair] = two_heads(turned[lanes])
        dot_ref[pair] = two_heads(turned_do[lanes])
        product = turned_do[lanes].astype(F32) * outt_ref[lanes, :].astype(F32)
        deltas.append(
            jnp.concatenate(
                [jnp.sum(product[:HD], axis=0, keepdims=True), jnp.sum(product[HD:], axis=0, keepdims=True)], axis=1
            )
        )
        for source, target in ((q_ref, q_split), (do_ref, do_split)):
            values = source[:, lanes].astype(F32)
            target[pair, :Q_TILE] = jnp.where(low_lanes, values, 0.0).astype(BF)
            target[pair, Q_TILE:] = jnp.where(low_lanes, 0.0, values).astype(BF)
    delta[...] = jnp.concatenate(deltas + [jnp.zeros((8 - H // 2, 2 * Q_TILE), F32)], axis=0)

    def tile(j, carry):
        @pl.when(flags[step * tiles + j] > 0)
        def _():
            keys = pl.ds(pl.multiple_of(j * K_TILE, K_TILE), K_TILE)
            bias = mask_tile(seg_col[keys, :], seg_row[...], bits_row[...], j * (K_TILE // block), block)
            bias = jnp.concatenate([bias, bias], axis=1)
            for pair in range(H // 2):
                lanes = slice(pair * 128, (pair + 1) * 128)
                row = slice(pair, pair + 1)
                scores = jnp.dot(k_ref[keys, lanes], qt[pair], preferred_element_type=F32) + bias
                prob = jnp.exp(scores - lse_ref[row, :])
                rise = jnp.dot(v_ref[keys, lanes], dot_ref[pair], preferred_element_type=F32)
                slope = (prob * (rise - delta[row, :])).astype(BF)
                product = jnp.dot(kt_ref[lanes, keys], slope, preferred_element_type=F32)
                dqt[lanes, :] = dqt[lanes, :] + own_columns(product)
                dv[keys, lanes] = dv[keys, lanes] + jnp.dot(
                    prob.astype(BF), do_split[pair], preferred_element_type=F32
                )
                dk[keys, lanes] = dk[keys, lanes] + jnp.dot(
                    slope, q_split[pair], preferred_element_type=F32
                )

        return carry

    lax.fori_loop(0, tiles, tile, 0)
    dq_ref[...] = (dqt[...] * HD**-0.5).T.astype(BF)

    @pl.when(step == pl.num_programs(0) - 1)
    def _():
        dk_ref[...] = (dk[...] * HD**-0.5).astype(BF)
        dv_ref[...] = dv[...].astype(BF)


def mask_tables(segments, chosen):
    length, blocks = segments.shape[0], chosen.shape[0]
    width = length // blocks
    ids = lax.iota(jnp.int32, blocks)
    open_blocks = jnp.any(chosen[:, :, None] == ids, axis=1) | (jnp.abs(ids[:, None] - ids) <= 1)
    bits = jnp.sum(jnp.where(open_blocks, lax.shift_left(jnp.ones_like(ids), ids), 0), axis=1)
    edges = segments.reshape(blocks, width)
    first, last = edges[:, 0], edges[:, -1]
    meet = open_blocks & (first[:, None] <= last[None]) & (first[None] <= last[:, None])
    rows, cols = Q_TILE // width, K_TILE // width
    tiles = meet.reshape(blocks // rows, rows, blocks // cols, cols)
    flags = jnp.any(tiles, axis=(1, 3)).astype(jnp.int32).reshape(-1)
    bits_row = jnp.repeat(bits, width)[None]
    return flags, segments[:, None], segments[None], bits_row


def whole(shape):
    return pl.BlockSpec(shape, lambda i, flags: (0,) * len(shape))


def row_tile(width):
    return pl.BlockSpec((Q_TILE, width), lambda i, flags: (i, 0))


def col_tile(height):
    return pl.BlockSpec((height, Q_TILE), lambda i, flags: (0, i))


def pair_tile():
    return pl.BlockSpec((8, 2 * Q_TILE), lambda i, flags: (0, i))


def attend(query, key, value_t, tables):
    flags, seg_col, seg_row, bits_row = tables
    length = query.shape[0]
    return pl.pallas_call(
        forward_kernel,
        out_shape=(
            jax.ShapeDtypeStruct((length, D), BF),
            jax.ShapeDtypeStruct((D, length), BF),
            jax.ShapeDtypeStruct((8, 2 * length), F32),
        ),
        grid_spec=pltpu.PrefetchScalarGridSpec(
            num_scalar_prefetch=1,
            grid=(length // Q_TILE,),
            in_specs=[
                row_tile(D), whole((length, D)), whole((D, length)), whole((length, 1)), col_tile(1), col_tile(1),
            ],
            out_specs=[row_tile(D), col_tile(D), pair_tile()],
            scratch_shapes=[
                pltpu.VMEM((H // 2, 128, 2 * Q_TILE), BF),
                pltpu.VMEM((8, 2 * Q_TILE), F32),
                pltpu.VMEM((8, 2 * Q_TILE), F32),
                pltpu.VMEM((D, Q_TILE), F32),
            ],
        ),
        compiler_params=pltpu.CompilerParams(vmem_limit_bytes=32 * 2**20),
        cost_estimate=pl.CostEstimate(
            flops=8 * length * length * D, bytes_accessed=10 * length * D, transcendentals=H * length * length
        ),
        name="attend",
    )(flags, query, key, value_t, seg_col, seg_row, bits_row)


def attend_back(query, key, key_t, value, grad, context_t, lse, tables):
    flags, seg_col, seg_row, bits_row = tables
    length = query.shape[0]
    return pl.pallas_call(
        backward_kernel,
        out_shape=tuple(jax.ShapeDtypeStruct((length, D), BF) for _ in range(3)),
        grid_spec=pltpu.PrefetchScalarGridSpec(
            num_scalar_prefetch=1,
            grid=(length // Q_TILE,),
            in_specs=[
                row_tile(D), whole((length, D)), whole((D, length)), whole((length, D)), row_tile(D), col_tile(D),
                pair_tile(), whole((length, 1)), col_tile(1), col_tile(1),
            ],
            out_specs=[row_tile(D), whole((length, D)), whole((length, D))],
            scratch_shapes=[
                pltpu.VMEM((H // 2, 128, 2 * Q_TILE), BF),
                pltpu.VMEM((H // 2, 128, 2 * Q_TILE), BF),
                pltpu.VMEM((H // 2, 2 * Q_TILE, 128), BF),
                pltpu.VMEM((H // 2, 2 * Q_TILE, 128), BF),
                pltpu.VMEM((8, 2 * Q_TILE), F32),
                pltpu.VMEM((D, Q_TILE), F32),
                pltpu.VMEM((length, D), F32),
                pltpu.VMEM((length, D), F32),
            ],
        ),
        compiler_params=pltpu.CompilerParams(vmem_limit_bytes=48 * 2**20),
        cost_estimate=pl.CostEstimate(
            flops=20 * length * length * D, bytes_accessed=18 * length * D, transcendentals=H * length * length
        ),
        name="attend_back",
    )(flags, query, key, key_t, value, grad, context_t, lse, seg_col, seg_row, bits_row)


def matmul(left, right):
    return jnp.dot(left, right, preferred_element_type=F32)


def contract_rows(left, right):
    return lax.dot_general(left, right, TN, preferred_element_type=F32)


def contract_cols(left, right):
    return lax.dot_general(left, right, NT, preferred_element_type=F32)


def column_sums(values):
    return jnp.sum(values.astype(F32), axis=0)


def normalize(residual, gain_row, shift_row):
    row_mean = jnp.mean(residual, axis=-1, keepdims=True)
    centered = residual - row_mean
    inverse = lax.rsqrt(jnp.mean(centered * centered, axis=-1, keepdims=True) + EPS)
    normed = centered * inverse
    return (normed * (1.0 + gain_row) + shift_row, normed, inverse)


def normalize_back(grad_out, normed, inverse, gain_row):
    grad_norm = grad_out * (1.0 + gain_row)
    centered = grad_norm - jnp.mean(grad_norm, axis=-1, keepdims=True)
    return inverse * (centered - normed * jnp.mean(grad_norm * normed, axis=-1, keepdims=True))


def attention(query, key, value, segment_ids, random_blocks):
    count, length = segment_ids.shape
    contexts, saved = [], []
    for s in range(count):
        part = slice(s * length, (s + 1) * length)
        tables = mask_tables(segment_ids[s], random_blocks[s])
        q, k, v = query[part], key[part], value[part]
        context, context_t, lse = attend(q, k, v.T, tables)
        contexts.append(context)
        saved.append((q, k, v, context_t, lse, tables))
    return jnp.concatenate(contexts), saved


def attention_back(saved, grad_context):
    length = grad_context.shape[0] // len(saved)
    parts = []
    for s, (q, k, v, context_t, lse, tables) in enumerate(saved):
        grad = grad_context[s * length : (s + 1) * length]
        parts.append(attend_back(q, k, k.T, v, grad, context_t, lse, tables))
    return [jnp.concatenate(part) for part in zip(*parts)]


def step_scale(rows, cols):
    return -MATRIX_RATE * math.sqrt(max(1.0, rows / cols))


def body(
    inputs,
    cotangent,
    segment_ids,
    random_blocks,
    qkv_weight,
    out_weight,
    up_weight,
    down_weight,
    vectors,
    ffn_bias,
    qkv_moment,
    out_moment,
    up_moment,
    down_moment,
    vector_moment,
    ffn_bias_moment,
):
    rep, shard = lax.axis_index("rep"), lax.axis_index("shard")
    shards = lax.axis_size("shard")
    core, plane = lax.rem(rep, 2), lax.rem(lax.div(rep, 2), 2)
    first_core = core == 0
    ff = ffn_bias.shape[0] * shards
    wide, unit = ffn_bias.shape[0] // 2, D // 2
    slim = D // shards

    def half_of(values, axis):
        size = values.shape[axis] // 2
        return lax.dynamic_slice_in_dim(values, core * size, size, axis)

    def ordered(mine, other, axis):
        low = jnp.where(first_core, mine, other)
        high = jnp.where(first_core, other, mine)
        return jnp.concatenate([low, high], axis)

    def swapped(values, axis):
        low, high = jnp.split(values, 2, axis)
        return ordered(low, high, axis)

    def gather_half(piece):
        mine = shard_gather(piece)
        mine = mine.reshape((-1,) + mine.shape[2:])
        return mine, flip(mine, "rep", 1)

    small = jnp.concatenate([vectors.reshape(1, -1), ffn_bias.reshape(1, -1)], axis=1)
    small = shard_gather(small).reshape(shards, -1).astype(F32)
    vec_rows = small[:, : 8 * slim].reshape(shards, 8, slim).swapaxes(0, 1).reshape(8, D)
    bias_ff = small[:, 8 * slim :].reshape(shards, 2, wide)
    bias_ff = swapped(bias_ff, 1).swapaxes(0, 1).reshape(ff)

    qkv_mine, qkv_other = gather_half(half_of(qkv_weight, 2).swapaxes(0, 1).reshape(slim, 3 * unit))
    out_mine, out_other = gather_half(half_of(out_weight, 1))
    up_piece = half_of(up_weight.reshape(slim, shards, 2, wide), 2).reshape(slim, ff // 2)
    up_mine, up_other = gather_half(up_piece)
    down_mine, down_other = gather_half(half_of(down_weight, 0))
    w_out = swapped(ordered(out_mine, out_other, 1), 0)
    w_up = jnp.concatenate([up_mine, up_other], axis=1)
    w_down = jnp.concatenate([down_mine, down_other], axis=0)

    scaling = HD ** (-0.5)
    both = jnp.concatenate([qkv_mine, qkv_other], axis=1)
    projected = matmul(inputs, both)
    bias_q, bias_v = swapped(vec_rows[0], 0), swapped(vec_rows[1], 0)

    def third(values, slot):
        return jnp.concatenate(
            [
                values[..., slot * unit : (slot + 1) * unit],
                values[..., (3 + slot) * unit : (4 + slot) * unit],
            ],
            axis=-1,
        )

    query_low = (third(projected, 0) + bias_q).astype(BF)
    key_low = third(projected, 1).astype(BF)
    value_low = (third(projected, 2) + bias_v).astype(BF)
    context_low, saved = attention(query_low, key_low, value_low, segment_ids, random_blocks)
    first = inputs.astype(F32) + matmul(context_low, w_out) + vec_rows[2]
    hidden, normed_one, inverse_one = normalize(first, vec_rows[3], vec_rows[4])
    hidden_low = hidden.astype(BF)
    pre_act = matmul(hidden_low, w_up) + bias_ff
    cumulative = 0.5 * (1.0 + lax.erf(pre_act * SQRT_HALF))
    act_low = (pre_act * cumulative).astype(BF)
    slope = (cumulative + pre_act * jnp.exp(-0.5 * pre_act * pre_act) * DENSITY_SCALE).astype(BF)
    second = hidden + matmul(act_low, w_down) + vec_rows[5]
    result, normed_two, inverse_two = normalize(second, vec_rows[6], vec_rows[7])
    outputs = result.astype(BF)

    grad_out = cotangent.astype(F32)
    grad_gain_two = jnp.sum(grad_out * normed_two, axis=0)
    grad_shift_two = jnp.sum(grad_out, axis=0)
    grad_second = normalize_back(grad_out, normed_two, inverse_two, vec_rows[6])
    grad_mlp = grad_second.astype(BF)
    grad_bias_down = column_sums(grad_mlp)
    down_part = contract_rows(act_low, grad_mlp).astype(BF).reshape(2, shards, wide, D)
    down_sums = reduce_halves(down_part[0], down_part[1])
    grad_pre = (contract_cols(grad_mlp, w_down) * slope.astype(F32)).astype(BF)
    grad_bias_up = column_sums(grad_pre)
    up_part = contract_rows(hidden_low, grad_pre).astype(BF).reshape(shards, slim, ff)
    up_sums = reduce_halves(up_part[..., : ff // 2], up_part[..., ff // 2 :])
    grad_hidden = grad_second + contract_cols(grad_pre, w_up)
    grad_gain_one = jnp.sum(grad_hidden * normed_one, axis=0)
    grad_shift_one = jnp.sum(grad_hidden, axis=0)
    grad_first = normalize_back(grad_hidden, normed_one, inverse_one, vec_rows[3])
    grad_att = grad_first.astype(BF)
    grad_bias_out = column_sums(grad_att)
    out_part = swapped(contract_rows(context_low, grad_att).astype(BF), 0)
    out_part = swapped(out_part, 1).reshape(shards, slim, D)
    out_sums = reduce_halves(out_part[..., :unit], out_part[..., unit:])
    grad_context = contract_cols(grad_att, w_out).astype(BF)
    grad_query, grad_key, grad_value = attention_back(saved, grad_context)

    def paired(half):
        part = slice(half * unit, (half + 1) * unit)
        return jnp.concatenate([grad_query[:, part], grad_key[:, part], grad_value[:, part]], axis=1)

    pairs = jnp.concatenate([paired(0), paired(1)], axis=1)
    qkv_part = contract_rows(inputs, pairs).astype(BF).reshape(shards, slim, 6 * unit)
    qkv_sums = reduce_halves(qkv_part[..., : 3 * unit], qkv_part[..., 3 * unit :])
    input_grad = grad_first + contract_cols(pairs, both)

    rows = [
        swapped(column_sums(grad_query), 0),
        swapped(column_sums(grad_value), 0),
        grad_bias_out,
        grad_gain_one,
        grad_shift_one,
        grad_bias_down,
        grad_gain_two,
        grad_shift_two,
    ]
    bias_rows = swapped(grad_bias_up.reshape(2, shards, wide), 0).swapaxes(0, 1).reshape(-1, D)
    totals = all_sum(jnp.concatenate([jnp.stack(rows), bias_rows]))
    vector_grad = lax.dynamic_slice_in_dim(totals[:8], shard * slim, slim, 1)
    ffn_bias_grad = lax.dynamic_slice_in_dim(totals[8:].reshape(ff), shard * 2 * wide, 2 * wide, 0)

    qkv_halves = [part.reshape(slim, 3, unit).swapaxes(0, 1) for part in qkv_sums]
    qkv_grad = ordered(qkv_halves[0], qkv_halves[1], 2)
    out_grad = ordered(out_sums[0], out_sums[1], 1)
    up_halves = [part.reshape(slim, shards, 1, wide) for part in up_sums]
    up_grad = ordered(up_halves[0], up_halves[1], 2).reshape(slim, ff)
    down_grad = ordered(down_sums[0], down_sums[1], 0)

    qkv_new = MOMENTUM * qkv_moment + qkv_grad
    out_new = MOMENTUM * out_moment + out_grad
    up_new = MOMENTUM * up_moment + up_grad
    down_new = MOMENTUM * down_moment + down_grad
    vector_new = MOMENTUM * vector_moment + vector_grad
    ffn_new = MOMENTUM * ffn_bias_moment + ffn_bias_grad

    groups = ff // D
    up_form = up_new.astype(BF).reshape(slim, groups, D).swapaxes(0, 1).reshape(2 * wide, D)
    tall = jnp.where(plane == 0, up_form, down_new.astype(BF))
    tall_mine = shard_gather(half_of(tall, 0))
    tall_blocks = ordered(tall_mine, flip(tall_mine, "rep", 1), 1)
    tall_mine = tall_step(tall_blocks, jnp.stack([shard, plane]).astype(jnp.int32))
    tall_other = flip(tall_mine, "rep", 2)
    up_piece = jnp.where(plane == 0, tall_mine, tall_other).astype(F32)
    down_piece = jnp.where(plane == 0, tall_other, tall_mine).astype(F32)
    up_update = step_scale(D, ff) * up_piece.reshape(groups, slim, D).swapaxes(0, 1).reshape(slim, ff)
    down_update = step_scale(ff, D) * down_piece

    turn = lax.rem(rep, 4)
    squares = jnp.concatenate([qkv_new, out_new[None]]).astype(BF)
    square = shard_gather(lax.dynamic_index_in_dim(squares, turn, 0, keepdims=False)).reshape(D, D)
    piece = square_step(square, shard[None].astype(jnp.int32))
    pieces = [piece, flip(piece, "rep", 1)]
    pieces = pieces + [flip(part, "rep", 2) for part in pieces]
    square_updates = jnp.stack(
        [lax.select_n(lax.bitwise_xor(turn, slot), *pieces) for slot in range(4)]
    )
    square_updates = step_scale(D, D) * square_updates.astype(F32)
    return (
        outputs,
        input_grad,
        qkv_grad,
        out_grad,
        up_grad,
        down_grad,
        vector_grad,
        ffn_bias_grad,
        qkv_new,
        out_new,
        up_new,
        down_new,
        vector_new,
        ffn_new,
        square_updates[:3],
        square_updates[3],
        up_update,
        down_update,
        -VECTOR_RATE * vector_new,
        -VECTOR_RATE * ffn_new,
    )


def solution(mesh):
    placed = (
        P(("rep", "shard"), None),
        P(("rep", "shard"), None),
        P(("rep", "shard"), None),
        P(("rep", "shard"), None, None),
        P(None, "shard", None),
        P("shard", None),
        P("shard", None),
        P("shard", None),
        P(None, "shard"),
        P("shard"),
        P(None, "shard", None),
        P("shard", None),
        P("shard", None),
        P("shard", None),
        P(None, "shard"),
        P("shard"),
    )
    return jax.shard_map(
        body,
        mesh=mesh,
        in_specs=placed,
        out_specs=(
            P(("rep", "shard"), None),
            P(("rep", "shard"), None),
            P(None, "shard", None),
            P("shard", None),
            P("shard", None),
            P("shard", None),
            P(None, "shard"),
            P("shard"),
            P(None, "shard", None),
            P("shard", None),
            P("shard", None),
            P("shard", None),
            P(None, "shard"),
            P("shard"),
            P(None, "shard", None),
            P("shard", None),
            P("shard", None),
            P("shard", None),
            P(None, "shard"),
            P("shard"),
        ),
        check_vma=False,
    )
```
